512 devices in a mesh: sec: 32 (over z, x), row: 16 (over y, core).
Axes of the slice: x: 4, y: 8, z: 8, core: 2. Of those that a mesh axis runs over, the one named last changes fastest.
Arguments:
- corner_ul: bfloat16 [32, 1024, 1024], P('sec', 'row'), may hold values from -6 to 6
- corner_ur: bfloat16 [32, 1024, 1024], P('sec'), may hold values from -0.1875 to 0.1875
- corner_dl: bfloat16 [32, 1024, 1024], P('sec', 'row'), may hold values from -6 to 6
- corner_dr: bfloat16 [32, 1024, 1024], P('sec'), may hold values from -0.1875 to 0.1875
- left_factor: bfloat16 [32, 1024, 16], P('sec', 'row'), may hold values from -0.1875 to 0.1875
- right_factor: bfloat16 [32, 1024, 16], P('sec', 'row'), may hold values from -0.1875 to 0.1875
- singular: float32 [32, 16], P('sec'), may hold values from 0.25 to 4
- states: int32 [32], P('sec'), may hold values from 8 to 16, as said below
- kept: int32 [32], P('sec'), may hold values from 8 to 16, as said below
- joining_map: int32 [32, 16], P('sec'), may hold values from 0 to 15, each once within a row
Outputs:
- proj_tilde: bfloat16 [32, 1024, 16], P('sec', 'row')
- proj: bfloat16 [32, 1024, 16], P('sec', 'row')
- intersection: float32 [32, 16, 16], P('sec')
The draws below stay inside these ranges and needn't reach their ends.
Inputs may be any that keep to these rules, and one draw needn't show every extreme that they name: `states`: at least half of 16; some sector has all 16. `kept`: at least half of 16; some sector keeps all 16. `joining_map`: each row is a permutation of 0 to 15.
All inputs are finite; a program needn't handle non-finite values.
Results may differ from the reference program's by a relative error of at most 0.0051.
Values may be sent and summed in bfloat16 or wider, within the bound.
A program may use at most 64 MiB of HBM per device.

```python
import math
import jax
import jax.numpy as jnp
from jax import lax

DD = 64
CHS = 16
KS = 16
DS = 1024
SECTORS = 32


def draw_states(key, part):
    first = jax.random.fold_in(key, 11)
    second = jax.random.fold_in(key, 12)
    values = jax.random.randint(first, (SECTORS,), (CHS + 1) // 2, CHS + 1)
    where_full = jax.random.randint(second, (), 0, SECTORS)
    return values.at[where_full].set(CHS).astype(jnp.int32)


def draw_kept(key, part):
    first = jax.random.fold_in(key, 21)
    second = jax.random.fold_in(key, 22)
    values = jax.random.randint(first, (SECTORS,), (KS + 1) // 2, KS + 1)
    where_full = jax.random.randint(second, (), 0, SECTORS)
    return values.at[where_full].set(KS).astype(jnp.int32)


def block_levels(key, dims, cuts, smallest, high):
    def one(dim, shards_of):
        steps = jax.random.uniform(jax.random.fold_in(jax.random.fold_in(key, 6), dim), (shards_of,), jnp.float32, smallest / len(cuts), high / len(cuts))
        return jnp.repeat(jnp.exp(steps), dims[dim] // shards_of).reshape((-1,) + (1,) * (len(dims) - dim - 1))

    gain = one(*cuts[0])
    for cut in cuts[1:]:
        gain = gain * one(*cut)
    return gain


def gaussian(rng, dims, width, bound, split=(), held_as=jnp.bfloat16):
    factor_of = block_levels(rng, dims, split, -0.22, 0.18) if split else 1.0
    result = jax.random.normal(rng, dims, jnp.float32) * width * factor_of
    return jnp.minimum(jnp.maximum(result, -bound), bound).astype(held_as)


def setup_inputs(seed: int = 0) -> dict:
    splits = jax.random.split(jax.random.key(seed), 11)
    return {
        "corner_ul": gaussian(splits[0], (SECTORS, DS, DS), 1.0, 6.0, ((0, 32), (1, 16))),
        "corner_ur": gaussian(splits[1], (SECTORS, DS, DS), DS ** -0.5, 0.1875, ((0, 32),)),
        "corner_dl": gaussian(splits[2], (SECTORS, DS, DS), 1.0, 6.0, ((0, 32), (1, 16))),
        "corner_dr": gaussian(splits[3], (SECTORS, DS, DS), DS ** -0.5, 0.1875, ((0, 32),)),
        "left_factor": gaussian(splits[4], (SECTORS, DS, KS), DS ** -0.5, 0.1875, ((0, 32), (1, 16))),
        "right_factor": gaussian(splits[5], (SECTORS, DS, KS), DS ** -0.5, 0.1875, ((0, 32), (1, 16))),
        "singular": jnp.clip(jnp.exp(math.log(4.0) - 2.7725887 * jax.random.uniform(splits[6], (SECTORS, KS), jnp.float32) ** block_levels(splits[6], (SECTORS, KS), ((0, 32),), -0.2, 0.2)), 0.25, 4.0),
        "states": draw_states(jax.random.fold_in(splits[10], 71), 0),
        "kept": draw_kept(jax.random.fold_in(splits[10], 71), 0),
        "joining_map": jax.vmap(lambda own: jax.random.permutation(own, CHS))(jax.random.split(splits[9], SECTORS)).reshape((SECTORS, CHS)).astype(jnp.int32),
    }


def regroup(block, order):
    four = block.reshape(DD, CHS, DD, CHS)
    four = jnp.take(four, order, axis=1)
    return jnp.transpose(four, (2, 1, 0, 3)).reshape(DS, DS)

def reference(corner_ul, corner_ur, corner_dl, corner_dr, left_factor, right_factor, singular, states, kept, joining_map):
    live_base = jnp.arange(DS, dtype=jnp.int32) % CHS

    def half(pieces):
        left, right, count = pieces
        live = (live_base < count).astype(jnp.float32)
        full = jnp.dot(left, right, preferred_element_type=jnp.float32)
        return (full * live[:, None] * live[None, :]).astype(jnp.bfloat16)
    upper = lax.map(half, (corner_ul, corner_ur, states))
    lower = lax.map(half, (corner_dl, corner_dr, states))
    sector_ids = jnp.arange(SECTORS, dtype=jnp.int32)

    def project(sector):
        up_src = upper[(sector - 1) % SECTORS]
        low_src = lower[(sector + 1) % SECTORS]
        r_left = regroup(up_src, joining_map[sector])
        r_right = regroup(low_src, joining_map[sector])
        a_half = jnp.dot(r_left.T, left_factor[sector], preferred_element_type=jnp.float32)
        b_half = jnp.dot(r_right.T, right_factor[sector], preferred_element_type=jnp.float32)
        columns = jnp.arange(KS, dtype=jnp.int32)
        weight = jnp.where(columns < kept[sector], 1.0 / jnp.sqrt(singular[sector]), 0.0).astype(jnp.float32)
        scaled_a = a_half * weight[None, :]
        scaled_b = b_half * weight[None, :]
        intersection = jnp.dot(scaled_a.T, scaled_b, precision=lax.Precision.HIGHEST, preferred_element_type=jnp.float32)
        intersection = intersection / jnp.sqrt(jnp.float32(DS))
        return (scaled_a.astype(jnp.bfloat16), scaled_b.astype(jnp.bfloat16), intersection)
    proj_tilde, proj, intersection = lax.map(project, sector_ids)
    return (proj_tilde, proj, intersection)
```

```python
import functools

import jax
import jax.numpy as jnp
from jax import lax
from jax.experimental import pallas as pl
from jax.experimental.pallas import tpu as pltpu
from jax.sharding import PartitionSpec as P

MESH = pl.DeviceIdType.MESH
F32 = jnp.float32
BF16 = jnp.bfloat16
LANES = 128
NT = (((1,), (1,)), ((), ()))


def kernel(
    n_sec, n_row,
    ul, ur, dl, dr, lf, rf, sg, st, kp, jm,
    pt, pj, it,
    v_left, v_right, v_fac, v_sg, v_jm, s_st, s_kp,
    gathered, outgoing, incoming, partial,
    big_sem, small_sem, g_send, g_recv, h_send, h_recv, i_send, i_recv,
):
    rows, width = ul.shape
    ks = lf.shape[0]
    chs = jm.shape[1]
    tiles = width // LANES
    chunk = 2 * LANES
    chunks = width // chunk
    sec = lax.axis_index("sec")
    row = lax.axis_index("row")
    near = (lax.rem(sec + 1, n_sec), lax.rem(sec + n_sec - 1, n_sec))
    y, core = row // 2, lax.rem(row, 2)
    n_y = n_row // 2
    steps = sorted(range(1, n_y), key=lambda d: -min(d, n_y - d))
    peers = [lax.rem(y + d, n_y) * 2 + c for d in steps for c in range(2)] + [y * 2 + 1 - core]

    lefts, rights = (ul, dl), (ur, dr)
    small = [
        pltpu.make_async_copy(lf, v_fac.at[pl.ds(0, ks)], small_sem.at[0]),
        pltpu.make_async_copy(rf, v_fac.at[pl.ds(ks, ks)], small_sem.at[1]),
        pltpu.make_async_copy(jm, v_jm, small_sem.at[2]),
        pltpu.make_async_copy(st, s_st, small_sem.at[3]),
        pltpu.make_async_copy(sg, v_sg, small_sem.at[4]),
        pltpu.make_async_copy(kp, s_kp, small_sem.at[5]),
    ]
    left_in = [pltpu.make_async_copy(lefts[h], v_left.at[h], small_sem.at[6 + h]) for h in range(2)]
    right_in = [
        [
            pltpu.make_async_copy(
                rights[h].at[:, pl.ds(c * chunk, chunk)],
                v_right.at[h, :, pl.ds(c * chunk, chunk)],
                big_sem.at[h, c],
            )
            for c in range(chunks)
        ]
        for h in range(2)
    ]
    for copy in small:
        copy.start()
    for h in range(2):
        left_in[h].start()
    for c in range(chunks):
        for h in range(2):
            right_in[h][c].start()

    barrier = pltpu.get_barrier_semaphore()
    for peer in peers:
        pl.semaphore_signal(barrier, inc=1, device_id={"row": peer}, device_id_type=MESH)
    for other in near:
        pl.semaphore_signal(barrier, inc=1, device_id={"sec": other}, device_id_type=MESH)

    for copy in small:
        copy.wait()

    seq = jnp.concatenate([v_jm[...]] * (rows // chs), axis=1)
    r64 = lax.broadcasted_iota(jnp.int32, (rows, rows), 0)
    c64 = lax.broadcasted_iota(jnp.int32, (rows, rows), 1)
    picker = jnp.where((r64 // chs == c64 // chs) & (lax.rem(r64, chs) == seq), 1.0, 0.0).astype(BF16)
    moved = lax.dot_general(v_fac[...], picker, NT, preferred_element_type=F32)
    gathered[row] = moved.astype(BF16)

    k_row = lax.broadcasted_iota(jnp.int32, (1, ks), 1)
    w_row = jnp.where(k_row < s_kp[0], 1.0 / jnp.sqrt(v_sg[...]), 0.0)
    rk = lax.broadcasted_iota(jnp.int32, (ks, ks), 0)
    ck = lax.broadcasted_iota(jnp.int32, (ks, ks), 1)
    weight = jnp.sum(jnp.where(rk == ck, jnp.broadcast_to(w_row, (ks, ks)), 0.0), axis=1, keepdims=True)

    states = s_st[0]
    lane = lax.broadcasted_iota(jnp.int32, (rows, LANES), 1)
    sub = lax.broadcasted_iota(jnp.int32, (rows, LANES), 0)
    live = (lax.rem(lane, chs) < states) & (lax.rem(sub, chs) < states)
    lane1 = lax.broadcasted_iota(jnp.int32, (2 * chs, LANES), 1)
    low2 = lax.rem(lane1 // (2 * chs), 2) == 0
    lane0 = lax.broadcasted_iota(jnp.int32, (chs, LANES), 1)
    low1 = lax.rem(lane0 // chs, 2) == 0

    def swap_blocks(tile):
        a, b = tile[: 2 * chs], tile[2 * chs :]
        ab = (
            jnp.where(low2, a, pltpu.roll(b, 2 * chs, 1)),
            jnp.where(low2, pltpu.roll(a, LANES - 2 * chs, 1), b),
        )
        out = []
        for half in ab:
            a, b = half[:chs], half[chs:]
            out.append(jnp.where(low1, a, pltpu.roll(b, chs, 1)))
            out.append(jnp.where(low1, pltpu.roll(a, LANES - chs, 1), b))
        return jnp.concatenate(out, axis=0)

    def half_copy(h, c):
        return pltpu.make_async_remote_copy(
            src_ref=outgoing.at[h, pl.ds(2 * c, 2)],
            dst_ref=incoming.at[h, pl.ds(2 * c, 2)],
            send_sem=h_send.at[h, c],
            recv_sem=h_recv.at[h, c],
            device_id={"sec": near[h]},
            device_id_type=MESH,
        )

    def compute(h, c):
        right_in[h][c].wait()
        full = jnp.dot(
            v_left[h], v_right[h, :, pl.ds(c * chunk, chunk)], preferred_element_type=F32
        )
        for i in range(2):
            tile = jnp.where(live, full[:, i * LANES : (i + 1) * LANES], 0.0)
            outgoing[h, 2 * c + i] = swap_blocks(tile).astype(BF16)

    for h in range(2):
        left_in[h].wait()
    for c in range(chunks):
        for h in range(2):
            compute(h, c)

    pl.semaphore_wait(barrier, n_row - 1 + 2)

    def gather_copy(slot, peer):
        return pltpu.make_async_remote_copy(
            src_ref=gathered.at[slot],
            dst_ref=gathered.at[slot],
            send_sem=g_send.at[peer],
            recv_sem=g_recv.at[slot],
            device_id={"row": peer},
            device_id_type=MESH,
        )

    for peer in peers:
        gather_copy(row, peer).start()
    for c in range(chunks):
        for h in range(2):
            half_copy(h, c).start()

    for peer in peers:
        gather_copy(peer, peer).wait_recv()

    halves = []
    for h in range(2):
        total = jnp.zeros((2 * ks, LANES), F32)
        for c in range(chunks):
            half_copy(h, c).wait_recv()
            for t in (2 * c, 2 * c + 1):
                lhs = jnp.concatenate(
                    [gathered[2 * t, pl.ds(h * ks, ks)], gathered[2 * t + 1, pl.ds(h * ks, ks)]], axis=0
                )
                total = total + jnp.dot(lhs, incoming[h, t], preferred_element_type=F32)
        halves.append((total[:ks, :rows] + total[ks:, rows:]) * weight)
    scaled_a, scaled_b = halves
    pt[...] = scaled_a.astype(BF16)
    pj[...] = scaled_b.astype(BF16)

    groups = LANES // ks
    wide = lax.dot_general(
        scaled_a,
        jnp.concatenate([scaled_b] * groups, axis=0),
        NT,
        precision=lax.Precision.HIGHEST,
        preferred_element_type=F32,
    )
    rw = lax.broadcasted_iota(jnp.int32, (ks, LANES), 0)
    cw = lax.broadcasted_iota(jnp.int32, (ks, LANES), 1)
    own = lax.rem(rw, groups) == cw // ks
    wide = jnp.where(own, wide, 0.0)
    for i in range(ks // groups):
        partial[row, pl.ds(i, 1)] = jnp.sum(wide[i * groups : (i + 1) * groups], axis=0, keepdims=True)

    def partial_copy(slot, peer):
        return pltpu.make_async_remote_copy(
            src_ref=partial.at[slot],
            dst_ref=partial.at[slot],
            send_sem=i_send.at[peer],
            recv_sem=i_recv.at[slot],
            device_id={"row": peer},
            device_id_type=MESH,
        )

    for peer in peers:
        partial_copy(row, peer).start()
    for peer in peers:
        gather_copy(row, peer).wait_send()
    for c in range(chunks):
        for h in range(2):
            half_copy(h, c).wait_send()
    for peer in peers:
        partial_copy(peer, peer).wait_recv()
    summed = partial[0]
    for i in range(1, n_row):
        summed = summed + partial[i]
    spread = jnp.concatenate(
        [jnp.broadcast_to(summed[i : i + 1], (groups, LANES)) for i in range(ks // groups)], axis=0
    )
    spread = jnp.where(own, spread, 0.0)
    shift = LANES // 2
    while shift >= ks:
        spread = spread + pltpu.roll(spread, shift, 1)
        shift //= 2
    it[...] = spread[:, :ks] / jnp.sqrt(F32(width))
    for peer in peers:
        partial_copy(row, peer).wait_send()


def local(
    corner_ul, corner_ur, corner_dl, corner_dr, left_factor, right_factor, singular, states, kept, joining_map
):
    n_sec, n_row = lax.axis_size("sec"), lax.axis_size("row")
    rows, width = corner_ul.shape[1:]
    ks = left_factor.shape[2]
    chs = joining_map.shape[1]
    tiles = width // LANES
    dma = pltpu.SemaphoreType.DMA
    pt, pj, it = pl.pallas_call(
        functools.partial(kernel, n_sec, n_row),
        out_shape=(
            jax.ShapeDtypeStruct((ks, rows), BF16),
            jax.ShapeDtypeStruct((ks, rows), BF16),
            jax.ShapeDtypeStruct((ks, ks), F32),
        ),
        in_specs=[pl.BlockSpec(memory_space=pl.ANY)] * 10,
        out_specs=(pl.BlockSpec(memory_space=pltpu.VMEM),) * 3,
        scratch_shapes=[
            pltpu.VMEM((2, rows, width), BF16),
            pltpu.VMEM((2, width, width), BF16),
            pltpu.VMEM((2 * ks, rows), BF16),
            pltpu.VMEM((1, ks), F32),
            pltpu.VMEM((1, chs), jnp.int32),
            pltpu.SMEM((1,), jnp.int32),
            pltpu.SMEM((1,), jnp.int32),
            pltpu.VMEM((n_row, 2 * ks, rows), BF16),
            pltpu.VMEM((2, tiles, rows, LANES), BF16),
            pltpu.VMEM((2, tiles, rows, LANES), BF16),
            pltpu.VMEM((n_row, ks * ks // LANES, LANES), F32),
            dma((2, 4)),
            dma((8,)),
            dma((n_row,)),
            dma((n_row,)),
            dma((2, 4)),
            dma((2, 4)),
            dma((n_row,)),
            dma((n_row,)),
        ],
        compiler_params=pltpu.CompilerParams(collective_id=0, has_side_effects=True),
    )(
        corner_ul[0], corner_ur[0], corner_dl[0], corner_dr[0],
        left_factor[0].T, right_factor[0].T,
        singular, states, kept, joining_map,
    )
    return pt.T[None], pj.T[None], it[None]


def solution(mesh):
    placed = (
        P("sec", "row", None),
        P("sec", None, None),
        P("sec", "row", None),
        P("sec", None, None),
        P("sec", "row", None),
        P("sec", "row", None),
        P("sec", None),
        P("sec"),
        P("sec"),
        P("sec", None),
    )
    return jax.shard_map(
        local,
        mesh=mesh,
        in_specs=placed,
        out_specs=(P("sec", "row", None), P("sec", "row", None), P("sec", None, None)),
        check_vma=False,
    )
```

```python
import functools

import jax
import jax.numpy as jnp
from jax import lax
from jax.experimental import pallas as pl
from jax.experimental.pallas import tpu as pltpu
from jax.sharding import PartitionSpec as P

MESH = pl.DeviceIdType.MESH
F32 = jnp.float32
BF16 = jnp.bfloat16
LANES = 128
NT = (((1,), (1,)), ((), ()))


def kernel(
    n_sec, n_row,
    ul, ur, dl, dr, lf, rf, sg, st, kp, jm,
    pt, pj, it,
    v_left, v_right, v_fac, v_sg, v_jm,
    gathered, outgoing, incoming, partial,
    big_sem, small_sem, g_send, g_recv, h_send, h_recv, i_send, i_recv,
):
    rows, width = ul.shape
    ks = lf.shape[0]
    chs = jm.shape[1]
    chunk = 2 * LANES
    chunks = width // chunk
    sec = lax.axis_index("sec")
    row = lax.axis_index("row")
    near = (lax.rem(sec + 1, n_sec), lax.rem(sec + n_sec - 1, n_sec))
    offsets = sorted(range(1, n_row), key=lambda d: -min(d, n_row - d))

    def peer(offset):
        return lax.rem(row + offset, n_row)

    lefts, rights = (ul, dl), (ur, dr)
    left_in = [pltpu.make_async_copy(lefts[h], v_left.at[h], small_sem.at[4 + h]) for h in range(2)]
    right_in = [
        [
            pltpu.make_async_copy(
                rights[h].at[:, pl.ds(c * chunk, chunk)],
                v_right.at[h, :, pl.ds(c * chunk, chunk)],
                big_sem.at[h, c],
            )
            for c in range(chunks)
        ]
        for h in range(2)
    ]
    small = [
        pltpu.make_async_copy(lf, v_fac.at[0], small_sem.at[0]),
        pltpu.make_async_copy(rf, v_fac.at[1], small_sem.at[1]),
        pltpu.make_async_copy(jm, v_jm, small_sem.at[2]),
        pltpu.make_async_copy(sg, v_sg, small_sem.at[3]),
    ]
    for copy in small:
        copy.start()
    for h in range(2):
        left_in[h].start()
    for c in range(chunks):
        for h in range(2):
            right_in[h][c].start()

    barrier = pltpu.get_barrier_semaphore()
    for other in near:
        pl.semaphore_signal(barrier, inc=1, device_id={"sec": other}, device_id_type=MESH)
    for offset in offsets:
        pl.semaphore_signal(barrier, inc=1, device_id={"row": peer(offset)}, device_id_type=MESH)

    def iota(shape, axis):
        return lax.broadcasted_iota(jnp.int32, shape, axis)

    r_pick, c_pick = iota((2 * rows, rows), 0), iota((2 * rows, rows), 1)
    same = lax.rem(r_pick, rows) // chs == c_pick // chs
    z_pick = lax.rem(r_pick, chs)
    left_rows = r_pick < rows
    states = st[0]
    lane, sub = iota((rows, LANES), 1), iota((rows, LANES), 0)
    live = (lax.rem(lane, chs) < states) & (lax.rem(sub, chs) < states)
    low2 = lax.rem(iota((2 * chs, LANES), 1) // (2 * chs), 2) == 0
    low1 = lax.rem(iota((chs, LANES), 1) // chs, 2) == 0

    for copy in small:
        copy.wait()
    seq = jnp.concatenate([v_jm[...]] * (rows // chs), axis=1)
    picker = jnp.where(same & (z_pick == seq), 1.0, 0.0)
    moved = lax.dot_general(
        v_fac[0], jnp.where(left_rows, picker, 0.0).astype(BF16), NT, preferred_element_type=F32
    ) + lax.dot_general(
        v_fac[1], jnp.where(left_rows, 0.0, picker).astype(BF16), NT, preferred_element_type=F32
    )
    gathered[0] = moved.astype(BF16)

    def swap_blocks(tile):
        a, b = tile[: 2 * chs], tile[2 * chs :]
        ab = (
            jnp.where(low2, a, pltpu.roll(b, 2 * chs, 1)),
            jnp.where(low2, pltpu.roll(a, LANES - 2 * chs, 1), b),
        )
        out = []
        for half in ab:
            a, b = half[:chs], half[chs:]
            out.append(jnp.where(low1, a, pltpu.roll(b, chs, 1)))
            out.append(jnp.where(low1, pltpu.roll(a, LANES - chs, 1), b))
        return jnp.concatenate(out, axis=0)

    def products(c):
        for h in range(2):
            right_in[h][c].wait()
        return [
            jnp.dot(v_left[h], v_right[h, :, pl.ds(c * chunk, chunk)], preferred_element_type=F32)
            for h in range(2)
        ]

    def finish(c, fulls):
        for h in range(2):
            for i in range(2):
                tile = jnp.where(live, fulls[h][:, i * LANES : (i + 1) * LANES], 0.0)
                outgoing[h, 2 * c + i] = swap_blocks(tile).astype(BF16)

    def half_copy(h, c):
        return pltpu.make_async_remote_copy(
            src_ref=outgoing.at[h, pl.ds(2 * c, 2)],
            dst_ref=incoming.at[pl.ds(2 * c, 2), pl.ds(h * rows, rows)],
            send_sem=h_send,
            recv_sem=h_recv.at[h, c],
            device_id={"sec": near[h]},
            device_id_type=MESH,
        )

    def row_copy(buffer, send_sem, recv_sem, offset):
        return pltpu.make_async_remote_copy(
            src_ref=buffer.at[0],
            dst_ref=buffer.at[n_row - offset],
            send_sem=send_sem,
            recv_sem=recv_sem,
            device_id={"row": peer(offset)},
            device_id_type=MESH,
        )

    def all_rows(buffer, send_sem, recv_sem):
        others = buffer.at[pl.ds(1, n_row - 1)]
        return pltpu.make_async_remote_copy(
            src_ref=others, dst_ref=others, send_sem=send_sem, recv_sem=recv_sem,
            device_id={"row": peer(1)}, device_id_type=MESH,
        )

    early = chunks // 2
    for h in range(2):
        left_in[h].wait()
    fulls = products(0)
    for c in range(1, early):
        following = products(c)
        finish(c - 1, fulls)
        fulls = following
    pl.semaphore_wait(barrier, n_row - 1 + 2)
    for offset in offsets:
        row_copy(gathered, g_send, g_recv, offset).start()
    for c in range(early - 1):
        for h in range(2):
            half_copy(h, c).start()
    for c in range(early, chunks + 1):
        following = products(c) if c < chunks else None
        finish(c - 1, fulls)
        for h in range(2):
            half_copy(h, c - 1).start()
        fulls = following

    w_row = jnp.where(iota((1, ks), 1) < kp[0], 1.0 / jnp.sqrt(v_sg[...]), 0.0)
    diagonal = iota((ks, ks), 0) == iota((ks, ks), 1)
    weight = jnp.sum(jnp.where(diagonal, jnp.broadcast_to(w_row, (ks, ks)), 0.0), axis=1, keepdims=True)

    all_rows(gathered, g_send, g_recv).wait_recv()
    upper_lanes = iota((2 * ks, LANES), 1) < rows
    zero = jnp.zeros((2 * ks, LANES), BF16)

    def factor(t):
        slots = [lax.rem(2 * t + g - row + n_row, n_row) for g in range(2)]
        both = jnp.concatenate([gathered[slot] for slot in slots], axis=0)
        return jnp.concatenate([jnp.where(upper_lanes, both, zero), jnp.where(upper_lanes, zero, both)], axis=0)

    total = jnp.zeros((4 * ks, LANES), F32)
    for c in range(chunks):
        lhs = jnp.concatenate([factor(2 * c), factor(2 * c + 1)], axis=1)
        for h in range(2):
            half_copy(h, c).wait_recv()
        rhs = incoming[pl.ds(2 * c, 2)].reshape(2 * LANES, LANES)
        total = total + jnp.dot(lhs, rhs, preferred_element_type=F32)
    scaled = [
        (total[2 * h * ks : (2 * h + 1) * ks, :rows] + total[(2 * h + 1) * ks : (2 * h + 2) * ks, rows:]) * weight
        for h in range(2)
    ]
    high = [v.astype(BF16) for v in scaled]
    low = [(v - u.astype(F32)).astype(BF16) for v, u in zip(scaled, high)]
    pt[...] = high[0]
    pj[...] = high[1]

    groups = LANES // ks
    wide = lax.dot_general(
        jnp.concatenate([high[0], low[0]], axis=0),
        jnp.concatenate([high[1]] * groups + [low[1]] * groups, axis=0),
        NT,
        preferred_element_type=F32,
    )
    wide = (wide[:ks, :LANES] + (wide[:ks, LANES:] + wide[ks:, :LANES])) + wide[ks:, LANES:]
    own = lax.rem(iota((ks, LANES), 0), groups) == iota((ks, LANES), 1) // ks
    wide = jnp.where(own, wide, 0.0)
    for i in range(ks // groups):
        partial[0, pl.ds(i, 1)] = jnp.sum(wide[i * groups : (i + 1) * groups], axis=0, keepdims=True)
    for offset in offsets:
        row_copy(partial, i_send, i_recv, offset).start()

    all_rows(gathered, g_send, g_recv).wait_send()
    pltpu.make_async_remote_copy(
        src_ref=outgoing, dst_ref=outgoing, send_sem=h_send, recv_sem=h_send,
        device_id={"sec": near[0]}, device_id_type=MESH,
    ).wait_send()
    all_rows(partial, i_send, i_recv).wait_recv()
    terms = [partial[i] for i in range(n_row)]
    while len(terms) > 1:
        terms = [a + b for a, b in zip(terms[::2], terms[1::2])]
    spread = jnp.concatenate(
        [jnp.broadcast_to(terms[0][i : i + 1], (groups, LANES)) for i in range(ks // groups)], axis=0
    )
    spread = jnp.where(own, spread, 0.0)
    shift = LANES // 2
    while shift >= ks:
        spread = spread + pltpu.roll(spread, shift, 1)
        shift //= 2
    it[...] = spread[:, :ks] / jnp.sqrt(F32(width))
    all_rows(partial, i_send, i_recv).wait_send()


def put_kernel(pt, pj, it, pt_out, pj_out, it_out, sem):
    copies = [
        pltpu.make_async_copy(a, b, sem.at[i])
        for i, (a, b) in enumerate(((pt, pt_out), (pj, pj_out), (it, it_out)))
    ]
    for copy in copies:
        copy.start()
    for copy in copies:
        copy.wait()


def local(
    corner_ul, corner_ur, corner_dl, corner_dr, left_factor, right_factor, singular, states, kept, joining_map
):
    n_sec, n_row = lax.axis_size("sec"), lax.axis_size("row")
    rows, width = corner_ul.shape[1:]
    ks = left_factor.shape[2]
    chs = joining_map.shape[1]
    tiles = width // LANES
    chunks = tiles // 2
    dma = pltpu.SemaphoreType.DMA
    hbm = pl.BlockSpec(memory_space=pltpu.HBM)
    smem = pl.BlockSpec(memory_space=pltpu.SMEM)
    vmem = pl.BlockSpec(memory_space=pltpu.VMEM)
    shapes = (((ks, rows), BF16), ((ks, rows), BF16), ((ks, ks), F32))
    results = pl.pallas_call(
        functools.partial(kernel, n_sec, n_row),
        out_shape=tuple(pltpu.VMEM(*s) for s in shapes),
        in_specs=[hbm] * 7 + [smem] * 2 + [hbm],
        out_specs=(vmem,) * 3,
        scratch_shapes=[
            pltpu.VMEM((2, rows, width), BF16),
            pltpu.VMEM((2, width, width), BF16),
            pltpu.VMEM((2, ks, rows), BF16),
            pltpu.VMEM((1, ks), F32),
            pltpu.VMEM((1, chs), jnp.int32),
            pltpu.VMEM((n_row, ks, 2 * rows), BF16),
            pltpu.VMEM((2, tiles, rows, LANES), BF16),
            pltpu.VMEM((tiles, 2 * rows, LANES), BF16),
            pltpu.VMEM((n_row, ks * ks // LANES, LANES), F32),
            dma((2, chunks)),
            dma((6,)),
            dma,
            dma,
            dma,
            dma((2, chunks)),
            dma,
            dma,
        ],
        compiler_params=pltpu.CompilerParams(collective_id=0, has_side_effects=True),
    )(
        corner_ul[0], corner_ur[0], corner_dl[0], corner_dr[0],
        left_factor[0].T, right_factor[0].T,
        singular, states, kept, joining_map,
    )
    pt, pj, it = pl.pallas_call(
        put_kernel,
        out_shape=tuple(jax.ShapeDtypeStruct(*s) for s in shapes),
        in_specs=[vmem] * 3,
        out_specs=(hbm,) * 3,
        scratch_shapes=[dma((3,))],
    )(*(pltpu.with_memory_space_constraint(v, pltpu.VMEM) for v in results))
    return pt.T[None], pj.T[None], it[None]


def solution(mesh):
    placed = (
        P("sec", "row", None),
        P("sec", None, None),
        P("sec", "row", None),
        P("sec", None, None),
        P("sec", "row", None),
        P("sec", "row", None),
        P("sec", None),
        P("sec"),
        P("sec"),
        P("sec", None),
    )
    return jax.shard_map(
        local,
        mesh=mesh,
        in_specs=placed,
        out_specs=(P("sec", "row", None), P("sec", "row", None), P("sec", None, None)),
        check_vma=False,
    )
```

```python
import functools

import jax
import jax.numpy as jnp
from jax import lax
from jax.experimental import pallas as pl
from jax.experimental.pallas import tpu as pltpu
from jax.sharding import PartitionSpec as P

MESH = pl.DeviceIdType.MESH
F32 = jnp.float32
BF16 = jnp.bfloat16
LANES = 128
NT = (((1,), (1,)), ((), ()))


def chunk_list(tiles):
    sizes = [2] * (tiles // 2)
    return [(sum(sizes[:i]), size) for i, size in enumerate(sizes)]


def kernel(
    n_sec, n_row,
    ul, ur, dl, dr, lf, rf, sg, st, kp, jm,
    pt, pj, it,
    v_left, v_right, v_fac, v_sg, v_jm,
    gathered, outgoing, incoming, partial,
    right_sem, left_sem, fac_sem, jm_sem, sg_sem, g_send, g_recv, h_send, h_recv, i_send, i_recv,
):
    rows, width = ul.shape
    ks = lf.shape[0]
    chs = jm.shape[1]
    tiles = width // LANES
    chunks = chunk_list(tiles)
    sec = lax.axis_index("sec")
    row = lax.axis_index("row")
    near = (lax.rem(sec + 1, n_sec), lax.rem(sec + n_sec - 1, n_sec))
    offsets = sorted(range(1, n_row), key=lambda d: -min(d, n_row - d))

    def peer(offset):
        return lax.rem(row + offset, n_row)

    lefts, rights, factors = (ul, dl), (ur, dr), (lf, rf)
    rounds = [[(h, i - h) for h in range(2) if 0 <= i - h < len(chunks)] for i in range(len(chunks) + 1)]

    def columns(c):
        return pl.ds(chunks[c][0] * LANES, chunks[c][1] * LANES)

    def left_in(h):
        return pltpu.make_async_copy(lefts[h], v_left.at[h], left_sem.at[h])

    def right_in(h, c):
        return pltpu.make_async_copy(
            rights[h].at[:, columns(c)], v_right.at[h, :, columns(c)], right_sem.at[h, c]
        )

    left_in(0).start()
    right_in(0, 0).start()
    barrier = pltpu.get_barrier_semaphore()
    for offset in offsets:
        pl.semaphore_signal(barrier, inc=1, device_id={"row": peer(offset)}, device_id_type=MESH)
    for other in near:
        pl.semaphore_signal(barrier, inc=1, device_id={"sec": other}, device_id_type=MESH)
    left_in(1).start()
    for h, c in rounds[1]:
        right_in(h, c).start()
    for h in range(2):
        pltpu.make_async_copy(factors[h], v_fac.at[h], fac_sem).start()
    jm_in = pltpu.make_async_copy(jm, v_jm, jm_sem)
    sg_in = pltpu.make_async_copy(sg, v_sg, sg_sem)
    jm_in.start()
    sg_in.start()

    def iota(shape, axis):
        return lax.broadcasted_iota(jnp.int32, shape, axis)

    r_pick, c_pick = iota((2 * rows, rows), 0), iota((2 * rows, rows), 1)
    same = lax.rem(r_pick, rows) // chs == c_pick // chs
    z_pick = lax.rem(r_pick, chs)
    left_rows = r_pick < rows
    states = st[0]
    lane, sub = iota((rows, LANES), 1), iota((rows, LANES), 0)
    live = (lax.rem(lane, chs) < states) & (lax.rem(sub, chs) < states)
    low2 = lax.rem(iota((2 * chs, LANES), 1) // (2 * chs), 2) == 0
    low1 = lax.rem(iota((chs, LANES), 1) // chs, 2) == 0

    def swap_blocks(tile):
        a, b = tile[: 2 * chs], tile[2 * chs :]
        ab = (
            jnp.where(low2, a, pltpu.roll(b, 2 * chs, 1)),
            jnp.where(low2, pltpu.roll(a, LANES - 2 * chs, 1), b),
        )
        out = []
        for half in ab:
            a, b = half[:chs], half[chs:]
            out.append(jnp.where(low1, a, pltpu.roll(b, chs, 1)))
            out.append(jnp.where(low1, pltpu.roll(a, LANES - chs, 1), b))
        return jnp.concatenate(out, axis=0)

    def own_factors():
        seq = jnp.concatenate([v_jm[...]] * (rows // chs), axis=1)
        picker = jnp.where(same & (z_pick == seq), 1.0, 0.0)
        moved = lax.dot_general(
            v_fac[0], jnp.where(left_rows, picker, 0.0).astype(BF16), NT, preferred_element_type=F32
        ) + lax.dot_general(
            v_fac[1], jnp.where(left_rows, 0.0, picker).astype(BF16), NT, preferred_element_type=F32
        )
        gathered[0] = moved.astype(BF16)

    def product(h, c):
        return jnp.dot(v_left[h], v_right[h, :, columns(c)], preferred_element_type=F32)

    def finish(h, c, full):
        for i in range(chunks[c][1]):
            tile = jnp.where(live, full[:, i * LANES : (i + 1) * LANES], 0.0)
            outgoing[h, chunks[c][0] + i] = swap_blocks(tile).astype(BF16)

    def half_copy(h, c):
        return pltpu.make_async_remote_copy(
            src_ref=outgoing.at[h, pl.ds(*chunks[c])],
            dst_ref=incoming.at[pl.ds(*chunks[c]), pl.ds(h * rows, rows)],
            send_sem=h_send,
            recv_sem=h_recv.at[h, c],
            device_id={"sec": near[h]},
            device_id_type=MESH,
        )

    def row_copy(buffer, send_sem, recv_sem, offset):
        return pltpu.make_async_remote_copy(
            src_ref=buffer.at[0],
            dst_ref=buffer.at[n_row - offset],
            send_sem=send_sem,
            recv_sem=recv_sem,
            device_id={"row": peer(offset)},
            device_id_type=MESH,
        )

    def all_rows(buffer, send_sem, recv_sem):
        others = buffer.at[pl.ds(1, n_row - 1)]
        return pltpu.make_async_remote_copy(
            src_ref=others, dst_ref=others, send_sem=send_sem, recv_sem=recv_sem,
            device_id={"row": peer(1)}, device_id_type=MESH,
        )

    for i, parts in enumerate(rounds):
        if i < 2:
            left_in(i).wait()
        for h, c in parts:
            right_in(h, c).wait()
        if i == 0:
            for later in rounds[2:]:
                for h, c in later:
                    right_in(h, c).start()
        if i == 1:
            pltpu.make_async_copy(v_fac, v_fac, fac_sem).wait()
            jm_in.wait()
        fulls = [product(h, c) for h, c in parts]
        if i == 1:
            own_factors()
        for (h, c), full in zip(parts, fulls):
            finish(h, c, full)
        if i == 0:
            pl.semaphore_wait(barrier, n_row - 1 + 2)
        for h, c in parts:
            half_copy(h, c).start()
        if i == 1:
            for offset in offsets:
                row_copy(gathered, g_send, g_recv, offset).start()

    sg_in.wait()
    w_row = jnp.where(iota((1, ks), 1) < kp[0], 1.0 / jnp.sqrt(v_sg[...]), 0.0)
    diagonal = iota((ks, ks), 0) == iota((ks, ks), 1)
    weight = jnp.sum(jnp.where(diagonal, jnp.broadcast_to(w_row, (ks, ks)), 0.0), axis=1, keepdims=True)

    all_rows(gathered, g_send, g_recv).wait_recv()
    upper_lanes = iota((2 * ks, LANES), 1) < rows
    zero = jnp.zeros((2 * ks, LANES), BF16)

    def factor(t):
        slots = [lax.rem(2 * t + g - row + n_row, n_row) for g in range(2)]
        both = jnp.concatenate([gathered[slot] for slot in slots], axis=0)
        return jnp.concatenate([jnp.where(upper_lanes, both, zero), jnp.where(upper_lanes, zero, both)], axis=0)

    total = jnp.zeros((4 * ks, LANES), F32)
    for c in range(len(chunks)):
        half_copy(1, c).wait_recv()
    for c, (first, count) in enumerate(chunks):
        lhs = jnp.concatenate([factor(first + i) for i in range(count)], axis=1)
        half_copy(0, c).wait_recv()
        rhs = incoming[pl.ds(first, count)].reshape(count * LANES, LANES)
        total = total + jnp.dot(lhs, rhs, preferred_element_type=F32)
    scaled = [
        (total[2 * h * ks : (2 * h + 1) * ks, :rows] + total[(2 * h + 1) * ks : (2 * h + 2) * ks, rows:]) * weight
        for h in range(2)
    ]
    high = [v.astype(BF16) for v in scaled]
    low = [(v - u.astype(F32)).astype(BF16) for v, u in zip(scaled, high)]
    pt[...] = high[0]
    pj[...] = high[1]

    groups = LANES // ks
    wide = lax.dot_general(
        jnp.concatenate([high[0], low[0]], axis=0),
        jnp.concatenate([high[1]] * groups + [low[1]] * groups, axis=0),
        NT,
        preferred_element_type=F32,
    )
    wide = (wide[:ks, :LANES] + (wide[:ks, LANES:] + wide[ks:, :LANES])) + wide[ks:, LANES:]
    own = lax.rem(iota((ks, LANES), 0) + iota((ks, LANES), 1) // ks, groups) == 0
    wide = jnp.where(own, wide, 0.0)
    for i in range(ks // groups):
        partial[0, pl.ds(i, 1)] = jnp.sum(wide[i * groups : (i + 1) * groups], axis=0, keepdims=True)
    for offset in offsets:
        row_copy(partial, i_send, i_recv, offset).start()

    all_rows(gathered, g_send, g_recv).wait_send()
    pltpu.make_async_remote_copy(
        src_ref=outgoing, dst_ref=outgoing, send_sem=h_send, recv_sem=h_send,
        device_id={"sec": near[0]}, device_id_type=MESH,
    ).wait_send()
    all_rows(partial, i_send, i_recv).wait_recv()
    terms = [partial[i] for i in range(n_row)]
    while len(terms) > 1:
        terms = [a + b for a, b in zip(terms[::2], terms[1::2])]
    spread = jnp.concatenate(
        [
            pltpu.roll(jnp.broadcast_to(terms[0][i : i + 1], (groups, LANES)), 0, 1, stride=ks, stride_axis=0)
            for i in range(ks // groups)
        ],
        axis=0,
    )
    it[...] = spread[:, :ks] / jnp.sqrt(F32(width))
    all_rows(partial, i_send, i_recv).wait_send()


def put_kernel(pt, pj, it, pt_out, pj_out, it_out, sem):
    copies = [
        pltpu.make_async_copy(a, b, sem.at[i])
        for i, (a, b) in enumerate(((pt, pt_out), (pj, pj_out), (it, it_out)))
    ]
    for copy in copies:
        copy.start()
    for copy in copies:
        copy.wait()


def local(
    corner_ul, corner_ur, corner_dl, corner_dr, left_factor, right_factor, singular, states, kept, joining_map
):
    n_sec, n_row = lax.axis_size("sec"), lax.axis_size("row")
    rows, width = corner_ul.shape[1:]
    ks = left_factor.shape[2]
    chs = joining_map.shape[1]
    tiles = width // LANES
    chunks = len(chunk_list(tiles))
    dma = pltpu.SemaphoreType.DMA
    hbm = pl.BlockSpec(memory_space=pltpu.HBM)
    smem = pl.BlockSpec(memory_space=pltpu.SMEM)
    vmem = pl.BlockSpec(memory_space=pltpu.VMEM)
    shapes = (((ks, rows), BF16), ((ks, rows), BF16), ((ks, ks), F32))
    results = pl.pallas_call(
        functools.partial(kernel, n_sec, n_row),
        out_shape=tuple(pltpu.VMEM(*s) for s in shapes),
        in_specs=[hbm] * 7 + [smem] * 2 + [hbm],
        out_specs=(vmem,) * 3,
        scratch_shapes=[
            pltpu.VMEM((2, rows, width), BF16),
            pltpu.VMEM((2, width, width), BF16),
            pltpu.VMEM((2, ks, rows), BF16),
            pltpu.VMEM((1, ks), F32),
            pltpu.VMEM((1, chs), jnp.int32),
            pltpu.VMEM((n_row, ks, 2 * rows), BF16),
            pltpu.VMEM((2, tiles, rows, LANES), BF16),
            pltpu.VMEM((tiles, 2 * rows, LANES), BF16),
            pltpu.VMEM((n_row, ks * ks // LANES, LANES), F32),
            dma((2, chunks)),
            dma((2,)),
            dma,
            dma,
            dma,
            dma,
            dma,
            dma,
            dma((2, chunks)),
            dma,
            dma,
        ],
        compiler_params=pltpu.CompilerParams(collective_id=0, has_side_effects=True),
    )(
        corner_ul[0], corner_ur[0], corner_dl[0], corner_dr[0],
        left_factor[0].T, right_factor[0].T,
        singular, states, kept, joining_map,
    )
    pt, pj, it = pl.pallas_call(
        put_kernel,
        out_shape=tuple(jax.ShapeDtypeStruct(*s) for s in shapes),
        in_specs=[vmem] * 3,
        out_specs=(hbm,) * 3,
        scratch_shapes=[dma((3,))],
    )(*(pltpu.with_memory_space_constraint(v, pltpu.VMEM) for v in results))
    return pt.T[None], pj.T[None], it[None]


def solution(mesh):
    placed = (
        P("sec", "row", None),
        P("sec", None, None),
        P("sec", "row", None),
        P("sec", None, None),
        P("sec", "row", None),
        P("sec", "row", None),
        P("sec", None),
        P("sec"),
        P("sec"),
        P("sec", None),
    )
    return jax.shard_map(
        local,
        mesh=mesh,
        in_specs=placed,
        out_specs=(P("sec", "row", None), P("sec", "row", None), P("sec", None, None)),
        check_vma=False,
    )
```

```python
import functools

import jax
import jax.numpy as jnp
from jax import lax
from jax.experimental import pallas as pl
from jax.experimental.pallas import tpu as pltpu
from jax.sharding import PartitionSpec as P

MESH = pl.DeviceIdType.MESH
F32 = jnp.float32
BF16 = jnp.bfloat16
LANES = 128
NT = (((1,), (1,)), ((), ()))


def chunk_list(tiles):
    sizes = [2] * (tiles // 2)
    return [(sum(sizes[:i]), size) for i, size in enumerate(sizes)]


def kernel(
    n_sec, n_row,
    ul, ur, dl, dr, lf, rf, sg, st, kp, jm,
    pt, pj, it,
    v_left, v_right, v_fac, v_sg, v_jm,
    gathered, outgoing, incoming, partial,
    right_sem, left_sem, fac_sem, jm_sem, sg_sem, g_send, g_recv, h_send, h_recv, i_send, i_recv,
):
    rows, width = ul.shape
    ks = lf.shape[0]
    chs = jm.shape[1]
    tiles = width // LANES
    chunks = chunk_list(tiles)
    sec = lax.axis_index("sec")
    row = lax.axis_index("row")
    near = (lax.rem(sec + 1, n_sec), lax.rem(sec + n_sec - 1, n_sec))
    offsets = sorted(range(1, n_row), key=lambda d: -min(d, n_row - d))

    def peer(offset):
        return lax.rem(row + offset, n_row)

    lefts, rights, factors = (ul, dl), (ur, dr), (lf, rf)
    rounds = [[(h, i - h) for h in range(2) if 0 <= i - h < len(chunks)] for i in range(len(chunks) + 1)]

    def columns(c):
        return pl.ds(chunks[c][0] * LANES, chunks[c][1] * LANES)

    def left_in(h):
        return pltpu.make_async_copy(lefts[h], v_left.at[h], left_sem.at[h])

    def held(h, tile, count):
        return pl.ds((tile + 2 * h) * LANES, count * LANES)

    def right_in(h, c):
        return pltpu.make_async_copy(
            rights[h].at[:, columns(c)], v_right.at[h, :, held(h, *chunks[c])], right_sem.at[c + h]
        )

    def round_in(parts):
        h, c = parts[0]
        landed = v_right.at[pl.ds(h, len(parts)), :, held(h, *chunks[c])]
        return pltpu.make_async_copy(landed, landed, right_sem.at[c + h])

    left_in(0).start()
    right_in(0, 0).start()
    barrier = pltpu.get_barrier_semaphore()
    for offset in offsets:
        pl.semaphore_signal(barrier, inc=1, device_id={"row": peer(offset)}, device_id_type=MESH)
    for other in near:
        pl.semaphore_signal(barrier, inc=1, device_id={"sec": other}, device_id_type=MESH)
    left_in(1).start()
    for h, c in rounds[1]:
        right_in(h, c).start()
    for h in range(2):
        pltpu.make_async_copy(factors[h], v_fac.at[h], fac_sem).start()
    jm_in = pltpu.make_async_copy(jm, v_jm, jm_sem)
    sg_in = pltpu.make_async_copy(sg, v_sg, sg_sem)
    jm_in.start()
    sg_in.start()

    def iota(shape, axis):
        return lax.broadcasted_iota(jnp.int32, shape, axis)

    r_pick, c_pick = iota((2 * rows, rows), 0), iota((2 * rows, rows), 1)
    same = lax.rem(r_pick, rows) // chs == c_pick // chs
    z_pick = lax.rem(r_pick, chs)
    left_rows = r_pick < rows
    states = st[0]
    lane, sub = iota((rows, LANES), 1), iota((rows, LANES), 0)
    live = (lax.rem(lane, chs) < states) & (lax.rem(sub, chs) < states)
    low2 = lax.rem(iota((2 * chs, LANES), 1) // (2 * chs), 2) == 0
    low1 = lax.rem(iota((chs, LANES), 1) // chs, 2) == 0

    def swap_blocks(tile):
        a, b = tile[: 2 * chs], tile[2 * chs :]
        ab = (
            jnp.where(low2, a, pltpu.roll(b, 2 * chs, 1)),
            jnp.where(low2, pltpu.roll(a, LANES - 2 * chs, 1), b),
        )
        out = []
        for half in ab:
            a, b = half[:chs], half[chs:]
            out.append(jnp.where(low1, a, pltpu.roll(b, chs, 1)))
            out.append(jnp.where(low1, pltpu.roll(a, LANES - chs, 1), b))
        return jnp.concatenate(out, axis=0)

    def own_factors():
        seq = jnp.concatenate([v_jm[...]] * (rows // chs), axis=1)
        picker = jnp.where(same & (z_pick == seq), 1.0, 0.0)
        moved = lax.dot_general(
            v_fac[0], jnp.where(left_rows, picker, 0.0).astype(BF16), NT, preferred_element_type=F32
        ) + lax.dot_general(
            v_fac[1], jnp.where(left_rows, 0.0, picker).astype(BF16), NT, preferred_element_type=F32
        )
        gathered[0] = moved.astype(BF16)

    def product(h, c, alone):
        if alone:
            first, count = chunks[c]
            return jnp.concatenate(
                [
                    jnp.dot(v_left[h], v_right[h, :, held(h, t, 1)], preferred_element_type=F32)
                    for t in range(first, first + count)
                ],
                axis=1,
            )
        return jnp.dot(v_left[h], v_right[h, :, held(h, *chunks[c])], preferred_element_type=F32)

    def finish(h, c, full):
        for i in range(chunks[c][1]):
            tile = jnp.where(live, full[:, i * LANES : (i + 1) * LANES], 0.0)
            outgoing[h, chunks[c][0] + i] = swap_blocks(tile).astype(BF16)

    last = len(chunks) - 1

    def arrival(h, c):
        return 0 if h else 1 + c // max(last, 1)

    def wait_half(h, first, count):
        landed = incoming.at[pl.ds(first, count), pl.ds(h * rows, rows)]
        pltpu.make_async_remote_copy(
            src_ref=landed, dst_ref=landed, send_sem=h_send, recv_sem=h_recv.at[arrival(h, first // 2)],
            device_id={"sec": near[h]}, device_id_type=MESH,
        ).wait_recv()

    def half_copy(h, c):
        return pltpu.make_async_remote_copy(
            src_ref=outgoing.at[h, pl.ds(*chunks[c])],
            dst_ref=incoming.at[pl.ds(*chunks[c]), pl.ds(h * rows, rows)],
            send_sem=h_send,
            recv_sem=h_recv.at[arrival(h, c)],
            device_id={"sec": near[h]},
            device_id_type=MESH,
        )

    def row_copy(buffer, send_sem, recv_sem, offset):
        return pltpu.make_async_remote_copy(
            src_ref=buffer.at[0],
            dst_ref=buffer.at[n_row - offset],
            send_sem=send_sem,
            recv_sem=recv_sem,
            device_id={"row": peer(offset)},
            device_id_type=MESH,
        )

    def all_rows(buffer, send_sem, recv_sem):
        others = buffer.at[pl.ds(1, n_row - 1)]
        return pltpu.make_async_remote_copy(
            src_ref=others, dst_ref=others, send_sem=send_sem, recv_sem=recv_sem,
            device_id={"row": peer(1)}, device_id_type=MESH,
        )

    for i, parts in enumerate(rounds):
        if i < 2:
            left_in(i).wait()
        round_in(parts).wait()
        if i == 0:
            for later in rounds[2:]:
                for h, c in later:
                    right_in(h, c).start()
        if i == 1:
            pltpu.make_async_copy(v_fac, v_fac, fac_sem).wait()
            jm_in.wait()
        fulls = [product(h, c, len(parts) == 1) for h, c in parts]
        if i == 1:
            own_factors()
        for (h, c), full in zip(parts, fulls):
            finish(h, c, full)
        if i == 0:
            pl.semaphore_wait(barrier, n_row - 1 + 2)
        for h, c in parts:
            half_copy(h, c).start()
        if i == 1:
            for offset in offsets:
                row_copy(gathered, g_send, g_recv, offset).start()

    sg_in.wait()
    w_row = jnp.where(iota((1, ks), 1) < kp[0], 1.0 / jnp.sqrt(v_sg[...]), 0.0)
    diagonal = iota((ks, ks), 0) == iota((ks, ks), 1)
    weight = jnp.sum(jnp.where(diagonal, jnp.broadcast_to(w_row, (ks, ks)), 0.0), axis=1, keepdims=True)

    all_rows(gathered, g_send, g_recv).wait_recv()
    upper_lanes = iota((2 * ks, LANES), 1) < rows

    def pair(t):
        a, b = (
            jnp.concatenate(
                [gathered[lax.rem(2 * i + g - row + n_row, n_row)].astype(F32) for g in range(2)], axis=0
            )
            for i in (t, t + 1)
        )
        return (
            jnp.where(upper_lanes, a, pltpu.roll(b, rows, 1)).astype(BF16),
            jnp.where(upper_lanes, pltpu.roll(a, rows, 1), b).astype(BF16),
        )

    pairs = [pair(first) for first, _ in chunks]

    def contract(h, c, total):
        first, count = chunks[c]
        rhs = incoming[pl.ds(first, count), pl.ds(h * rows, rows)].reshape(count * rows, LANES)
        return total + jnp.dot(pairs[c][h], rhs, preferred_element_type=F32)

    def parted(total):
        return jnp.where(upper_lanes[:ks], total[:ks], total[ks:]) * weight

    def folded(value):
        return value + pltpu.roll(value, rows, 1)

    def split(value):
        high = value.astype(BF16)
        return high, (value - high.astype(F32)).astype(BF16)

    totals = [jnp.zeros((2 * ks, LANES), F32)] * 2
    wait_half(1, 0, tiles)
    for c in range(len(chunks)):
        totals[1] = contract(1, c, totals[1])
    scaled_b = folded(parted(totals[1]))
    pj[...] = scaled_b[:, :rows].astype(BF16)
    groups = LANES // ks
    high_b, low_b = (jnp.concatenate([v] * groups, axis=0) for v in split(scaled_b))
    rhs_b = jnp.concatenate([high_b, low_b, high_b], axis=1)
    wait_half(0, 0, tiles - 2)
    for c in range(len(chunks)):
        if c == last:
            wait_half(0, tiles - 2, 2)
        totals[0] = contract(0, c, totals[0])
    parted_a = parted(totals[0])

    high_a, low_a = split(parted_a)
    wide = lax.dot_general(
        jnp.concatenate([high_a, high_a, low_a], axis=1), rhs_b, NT, preferred_element_type=F32
    )
    own = lax.rem(iota((ks, LANES), 0) + iota((ks, LANES), 1) // ks, groups) == 0
    wide = jnp.where(own, wide, 0.0)
    for i in range(ks // groups):
        partial[0, pl.ds(i, 1)] = jnp.sum(wide[i * groups : (i + 1) * groups], axis=0, keepdims=True)
    for offset in offsets:
        row_copy(partial, i_send, i_recv, offset).start()

    pt[...] = folded(parted_a)[:, :rows].astype(BF16)
    all_rows(gathered, g_send, g_recv).wait_send()
    pltpu.make_async_remote_copy(
        src_ref=outgoing, dst_ref=outgoing, send_sem=h_send, recv_sem=h_send,
        device_id={"sec": near[0]}, device_id_type=MESH,
    ).wait_send()
    all_rows(partial, i_send, i_recv).wait_recv()
    terms = [partial[i] for i in range(n_row)]
    while len(terms) > 1:
        terms = [a + b for a, b in zip(terms[::2], terms[1::2])]
    spread = jnp.concatenate(
        [
            pltpu.roll(jnp.broadcast_to(terms[0][i : i + 1], (groups, LANES)), 0, 1, stride=ks, stride_axis=0)
            for i in range(ks // groups)
        ],
        axis=0,
    )
    it[...] = spread[:, :ks] / jnp.sqrt(F32(width))
    all_rows(partial, i_send, i_recv).wait_send()


def put_kernel(pt, pj, it, pt_out, pj_out, it_out, sem):
    copies = [
        pltpu.make_async_copy(a, b, sem.at[i])
        for i, (a, b) in enumerate(((pt, pt_out), (pj, pj_out), (it, it_out)))
    ]
    for copy in copies:
        copy.start()
    for copy in copies:
        copy.wait()


def local(
    corner_ul, corner_ur, corner_dl, corner_dr, left_factor, right_factor, singular, states, kept, joining_map
):
    n_sec, n_row = lax.axis_size("sec"), lax.axis_size("row")
    rows, width = corner_ul.shape[1:]
    ks = left_factor.shape[2]
    chs = joining_map.shape[1]
    tiles = width // LANES
    chunks = len(chunk_list(tiles))
    dma = pltpu.SemaphoreType.DMA
    hbm = pl.BlockSpec(memory_space=pltpu.HBM)
    smem = pl.BlockSpec(memory_space=pltpu.SMEM)
    vmem = pl.BlockSpec(memory_space=pltpu.VMEM)
    shapes = (((ks, rows), BF16), ((ks, rows), BF16), ((ks, ks), F32))
    results = pl.pallas_call(
        functools.partial(kernel, n_sec, n_row),
        out_shape=tuple(pltpu.VMEM(*s) for s in shapes),
        in_specs=[hbm] * 7 + [smem] * 2 + [hbm],
        out_specs=(vmem,) * 3,
        scratch_shapes=[
            pltpu.VMEM((2, rows, width), BF16),
            pltpu.VMEM((2, width, width + 2 * LANES), BF16),
            pltpu.VMEM((2, ks, rows), BF16),
            pltpu.VMEM((1, ks), F32),
            pltpu.VMEM((1, chs), jnp.int32),
            pltpu.VMEM((n_row, ks, 2 * rows), BF16),
            pltpu.VMEM((2, tiles, rows, LANES), BF16),
            pltpu.VMEM((tiles, 2 * rows, LANES), BF16),
            pltpu.VMEM((n_row, ks * ks // LANES, LANES), F32),
            dma((chunks + 1,)),
            dma((2,)),
            dma,
            dma,
            dma,
            dma,
            dma,
            dma,
            dma((3,)),
            dma,
            dma,
        ],
        compiler_params=pltpu.CompilerParams(collective_id=0, has_side_effects=True),
    )(
        corner_ul[0], corner_ur[0], corner_dl[0], corner_dr[0],
        left_factor[0].T, right_factor[0].T,
        singular, states, kept, joining_map,
    )
    pt, pj, it = pl.pallas_call(
        put_kernel,
        out_shape=tuple(jax.ShapeDtypeStruct(*s) for s in shapes),
        in_specs=[vmem] * 3,
        out_specs=(hbm,) * 3,
        scratch_shapes=[dma((3,))],
    )(*(pltpu.with_memory_space_constraint(v, pltpu.VMEM) for v in results))
    return pt.T[None], pj.T[None], it[None]


def solution(mesh):
    placed = (
        P("sec", "row", None),
        P("sec", None, None),
        P("sec", "row", None),
        P("sec", None, None),
        P("sec", "row", None),
        P("sec", "row", None),
        P("sec", None),
        P("sec"),
        P("sec"),
        P("sec", None),
    )
    return jax.shard_map(
        local,
        mesh=mesh,
        in_specs=placed,
        out_specs=(P("sec", "row", None), P("sec", "row", None), P("sec", None, None)),
        check_vma=False,
    )
```

```python
import functools

import jax
import jax.numpy as jnp
from jax import lax
from jax.experimental import pallas as pl
from jax.experimental.pallas import tpu as pltpu
from jax.sharding import PartitionSpec as P

MESH = pl.DeviceIdType.MESH
F32 = jnp.float32
BF16 = jnp.bfloat16
LANES = 128
NT = (((1,), (1,)), ((), ()))


def chunk_list(tiles):
    sizes = [2] * (tiles // 2)
    return [(sum(sizes[:i]), size) for i, size in enumerate(sizes)]


def kernel(
    n_sec, n_row,
    ul, ur, dl, dr, lf, rf, sg, st, kp, jm,
    pt, pj, it,
    v_left, v_right, v_fac, v_sg, v_jm,
    gathered, outgoing, incoming, partial,
    right_sem, left_sem, fac_sem, jm_sem, sg_sem, g_send, g_recv, h_send, h_recv, i_send, i_recv,
):
    rows, width = ul.shape
    ks = lf.shape[0]
    chs = jm.shape[1]
    tiles = width // LANES
    chunks = chunk_list(tiles)
    sec = lax.axis_index("sec")
    row = lax.axis_index("row")
    near = (lax.rem(sec + 1, n_sec), lax.rem(sec + n_sec - 1, n_sec))
    offsets = sorted(range(1, n_row), key=lambda d: -min(d, n_row - d))

    def peer(offset):
        return lax.rem(row + offset, n_row)

    lefts, rights, factors = (ul, dl), (ur, dr), (lf, rf)
    rounds = [[(h, i - h) for h in range(2) if 0 <= i - h < len(chunks)] for i in range(len(chunks) + 1)]

    def columns(c):
        return pl.ds(chunks[c][0] * LANES, chunks[c][1] * LANES)

    def left_in(h):
        return pltpu.make_async_copy(lefts[h], v_left.at[h], left_sem.at[h])

    def held(h, tile, count):
        return pl.ds((tile + 2 * h) * LANES, count * LANES)

    def right_in(h, c):
        return pltpu.make_async_copy(
            rights[h].at[:, columns(c)], v_right.at[h, :, held(h, *chunks[c])], right_sem.at[c + h]
        )

    def round_in(parts):
        h, c = parts[0]
        landed = v_right.at[pl.ds(h, len(parts)), :, held(h, *chunks[c])]
        return pltpu.make_async_copy(landed, landed, right_sem.at[c + h])

    left_in(0).start()
    right_in(0, 0).start()
    barrier = pltpu.get_barrier_semaphore()
    for offset in offsets:
        pl.semaphore_signal(barrier, inc=1, device_id={"row": peer(offset)}, device_id_type=MESH)
    for other in near:
        pl.semaphore_signal(barrier, inc=1, device_id={"sec": other}, device_id_type=MESH)
    left_in(1).start()
    for h, c in rounds[1]:
        right_in(h, c).start()
    for h in range(2):
        pltpu.make_async_copy(factors[h], v_fac.at[h], fac_sem).start()
    jm_in = pltpu.make_async_copy(jm, v_jm, jm_sem)
    sg_in = pltpu.make_async_copy(sg, v_sg, sg_sem)
    jm_in.start()
    sg_in.start()

    def iota(shape, axis):
        return lax.broadcasted_iota(jnp.int32, shape, axis)

    r_pick, c_pick = iota((2 * rows, rows), 0), iota((2 * rows, rows), 1)
    same = lax.rem(r_pick, rows) // chs == c_pick // chs
    z_pick = lax.rem(r_pick, chs)
    left_rows = r_pick < rows
    states = st[0]
    lane, sub = iota((rows, LANES), 1), iota((rows, LANES), 0)
    live = (lax.rem(lane, chs) < states) & (lax.rem(sub, chs) < states)
    low2 = lax.rem(iota((2 * chs, LANES), 1) // (2 * chs), 2) == 0
    low1 = lax.rem(iota((chs, LANES), 1) // chs, 2) == 0

    def swap_blocks(tile):
        a, b = tile[: 2 * chs], tile[2 * chs :]
        ab = (
            jnp.where(low2, a, pltpu.roll(b, 2 * chs, 1)),
            jnp.where(low2, pltpu.roll(a, LANES - 2 * chs, 1), b),
        )
        out = []
        for half in ab:
            a, b = half[:chs], half[chs:]
            out.append(jnp.where(low1, a, pltpu.roll(b, chs, 1)))
            out.append(jnp.where(low1, pltpu.roll(a, LANES - chs, 1), b))
        return jnp.concatenate(out, axis=0)

    def own_factors():
        seq = jnp.concatenate([v_jm[...]] * (rows // chs), axis=1)
        picker = jnp.where(same & (z_pick == seq), 1.0, 0.0)
        moved = lax.dot_general(
            v_fac[0], jnp.where(left_rows, picker, 0.0).astype(BF16), NT, preferred_element_type=F32
        ) + lax.dot_general(
            v_fac[1], jnp.where(left_rows, 0.0, picker).astype(BF16), NT, preferred_element_type=F32
        )
        gathered[0] = moved.astype(BF16)

    def product(h, c, alone):
        if alone:
            first, count = chunks[c]
            return jnp.concatenate(
                [
                    jnp.dot(v_left[h], v_right[h, :, held(h, t, 1)], preferred_element_type=F32)
                    for t in range(first, first + count)
                ],
                axis=1,
            )
        return jnp.dot(v_left[h], v_right[h, :, held(h, *chunks[c])], preferred_element_type=F32)

    def finish(h, c, full):
        for i in range(chunks[c][1]):
            tile = jnp.where(live, full[:, i * LANES : (i + 1) * LANES], 0.0)
            outgoing[h, chunks[c][0] + i] = swap_blocks(tile).astype(BF16)

    last = len(chunks) - 1

    def arrival(h, c):
        return 0 if h else 1 + c // max(last, 1)

    def wait_half(h, first, count):
        landed = incoming.at[pl.ds(first, count), pl.ds(h * rows, rows)]
        pltpu.make_async_remote_copy(
            src_ref=landed, dst_ref=landed, send_sem=h_send, recv_sem=h_recv.at[arrival(h, first // 2)],
            device_id={"sec": near[h]}, device_id_type=MESH,
        ).wait_recv()

    def half_copy(h, c):
        return pltpu.make_async_remote_copy(
            src_ref=outgoing.at[h, pl.ds(*chunks[c])],
            dst_ref=incoming.at[pl.ds(*chunks[c]), pl.ds(h * rows, rows)],
            send_sem=h_send,
            recv_sem=h_recv.at[arrival(h, c)],
            device_id={"sec": near[h]},
            device_id_type=MESH,
        )

    def row_copy(buffer, send_sem, recv_sem, offset):
        return pltpu.make_async_remote_copy(
            src_ref=buffer.at[0],
            dst_ref=buffer.at[n_row - offset],
            send_sem=send_sem,
            recv_sem=recv_sem,
            device_id={"row": peer(offset)},
            device_id_type=MESH,
        )

    def all_rows(buffer, send_sem, recv_sem):
        others = buffer.at[pl.ds(1, n_row - 1)]
        return pltpu.make_async_remote_copy(
            src_ref=others, dst_ref=others, send_sem=send_sem, recv_sem=recv_sem,
            device_id={"row": peer(1)}, device_id_type=MESH,
        )

    for i, parts in enumerate(rounds):
        if i < 2:
            left_in(i).wait()
        round_in(parts).wait()
        if i == 0:
            for later in rounds[2:]:
                for h, c in later:
                    right_in(h, c).start()
        if i == 1:
            pltpu.make_async_copy(v_fac, v_fac, fac_sem).wait()
            jm_in.wait()
        fulls = [product(h, c, len(parts) == 1) for h, c in parts]
        if i == 1:
            own_factors()
        for (h, c), full in zip(parts, fulls):
            finish(h, c, full)
        if i == 0:
            pl.semaphore_wait(barrier, n_row - 1 + 2)
        for h, c in parts:
            half_copy(h, c).start()
        if i == 1:
            for offset in offsets:
                row_copy(gathered, g_send, g_recv, offset).start()

    sg_in.wait()
    w_row = jnp.where(iota((1, ks), 1) < kp[0], 1.0 / jnp.sqrt(v_sg[...]), 0.0)
    diagonal = iota((ks, ks), 0) == iota((ks, ks), 1)
    weight = jnp.sum(jnp.where(diagonal, jnp.broadcast_to(w_row, (ks, ks)), 0.0), axis=1, keepdims=True)

    all_rows(gathered, g_send, g_recv).wait_recv()
    upper_lanes = iota((2 * ks, LANES), 1) < rows

    def pair(t):
        a, b = (
            jnp.concatenate(
                [gathered[lax.rem(2 * i + g - row + n_row, n_row)].astype(F32) for g in range(2)], axis=0
            )
            for i in (t, t + 1)
        )
        return (
            jnp.where(upper_lanes, a, pltpu.roll(b, rows, 1)).astype(BF16),
            jnp.where(upper_lanes, pltpu.roll(a, rows, 1), b).astype(BF16),
        )

    pairs = [pair(first) for first, _ in chunks]

    def contract(h, c, total):
        first, count = chunks[c]
        rhs = incoming[pl.ds(first, count), pl.ds(h * rows, rows)].reshape(count * rows, LANES)
        return total + jnp.dot(pairs[c][h], rhs, preferred_element_type=F32)

    def parted(total):
        return jnp.where(upper_lanes[:ks], total[:ks], total[ks:]) * weight

    def folded(value):
        return value + pltpu.roll(value, rows, 1)

    def split(value):
        high = value.astype(BF16)
        return high, (value - high.astype(F32)).astype(BF16)

    totals = [jnp.zeros((2 * ks, LANES), F32)] * 2
    wait_half(1, 0, tiles)
    for c in range(len(chunks)):
        totals[1] = contract(1, c, totals[1])
    scaled_b = folded(parted(totals[1]))
    pj[...] = scaled_b[:, :rows].astype(BF16)
    groups = LANES // ks
    high_b, low_b = (jnp.concatenate([v] * groups, axis=0) for v in split(scaled_b))
    rhs_b = jnp.concatenate([high_b, low_b, high_b, low_b], axis=1)
    wait_half(0, 0, tiles - 2)
    for c in range(len(chunks)):
        if c == last:
            wait_half(0, tiles - 2, 2)
        totals[0] = contract(0, c, totals[0])
    parted_a = parted(totals[0])

    high_a, low_a = split(parted_a)
    wide = lax.dot_general(
        jnp.concatenate([high_a, high_a, low_a, low_a], axis=1), rhs_b, NT, preferred_element_type=F32
    )
    own = lax.rem(iota((ks, LANES), 0) + iota((ks, LANES), 1) // ks, groups) == 0
    wide = jnp.where(own, wide, 0.0)
    for i in range(ks // groups):
        partial[0, pl.ds(i, 1)] = jnp.sum(wide[i * groups : (i + 1) * groups], axis=0, keepdims=True)
    for offset in offsets:
        row_copy(partial, i_send, i_recv, offset).start()

    pt[...] = folded(parted_a)[:, :rows].astype(BF16)
    all_rows(gathered, g_send, g_recv).wait_send()
    pltpu.make_async_remote_copy(
        src_ref=outgoing, dst_ref=outgoing, send_sem=h_send, recv_sem=h_send,
        device_id={"sec": near[0]}, device_id_type=MESH,
    ).wait_send()
    all_rows(partial, i_send, i_recv).wait_recv()
    terms = [partial[i] for i in range(n_row)]
    while len(terms) > 1:
        terms = [a + b for a, b in zip(terms[::2], terms[1::2])]
    spread = jnp.concatenate(
        [
            pltpu.roll(jnp.broadcast_to(terms[0][i : i + 1], (groups, LANES)), 0, 1, stride=ks, stride_axis=0)
            for i in range(ks // groups)
        ],
        axis=0,
    )
    it[...] = spread[:, :ks] / jnp.sqrt(F32(width))
    all_rows(partial, i_send, i_recv).wait_send()


def put_kernel(pt, pj, it, pt_out, pj_out, it_out, sem):
    copies = [
        pltpu.make_async_copy(a, b, sem.at[i])
        for i, (a, b) in enumerate(((pt, pt_out), (pj, pj_out), (it, it_out)))
    ]
    for copy in copies:
        copy.start()
    for copy in copies:
        copy.wait()


def local(
    corner_ul, corner_ur, corner_dl, corner_dr, left_factor, right_factor, singular, states, kept, joining_map
):
    n_sec, n_row = lax.axis_size("sec"), lax.axis_size("row")
    rows, width = corner_ul.shape[1:]
    ks = left_factor.shape[2]
    chs = joining_map.shape[1]
    tiles = width // LANES
    chunks = len(chunk_list(tiles))
    dma = pltpu.SemaphoreType.DMA
    hbm = pl.BlockSpec(memory_space=pltpu.HBM)
    smem = pl.BlockSpec(memory_space=pltpu.SMEM)
    vmem = pl.BlockSpec(memory_space=pltpu.VMEM)
    shapes = (((ks, rows), BF16), ((ks, rows), BF16), ((ks, ks), F32))
    results = pl.pallas_call(
        functools.partial(kernel, n_sec, n_row),
        out_shape=tuple(pltpu.VMEM(*s) for s in shapes),
        in_specs=[hbm] * 7 + [smem] * 2 + [hbm],
        out_specs=(vmem,) * 3,
        scratch_shapes=[
            pltpu.VMEM((2, rows, width), BF16),
            pltpu.VMEM((2, width, width + 2 * LANES), BF16),
            pltpu.VMEM((2, ks, rows), BF16),
            pltpu.VMEM((1, ks), F32),
            pltpu.VMEM((1, chs), jnp.int32),
            pltpu.VMEM((n_row, ks, 2 * rows), BF16),
            pltpu.VMEM((2, tiles, rows, LANES), BF16),
            pltpu.VMEM((tiles, 2 * rows, LANES), BF16),
            pltpu.VMEM((n_row, ks * ks // LANES, LANES), F32),
            dma((chunks + 1,)),
            dma((2,)),
            dma,
            dma,
            dma,
            dma,
            dma,
            dma,
            dma((3,)),
            dma,
            dma,
        ],
        compiler_params=pltpu.CompilerParams(collective_id=0, has_side_effects=True),
    )(
        corner_ul[0], corner_ur[0], corner_dl[0], corner_dr[0],
        left_factor[0].T, right_factor[0].T,
        singular, states, kept, joining_map,
    )
    pt, pj, it = pl.pallas_call(
        put_kernel,
        out_shape=tuple(jax.ShapeDtypeStruct(*s) for s in shapes),
        in_specs=[vmem] * 3,
        out_specs=(hbm,) * 3,
        scratch_shapes=[dma((3,))],
    )(*(pltpu.with_memory_space_constraint(v, pltpu.VMEM) for v in results))
    return pt.T[None], pj.T[None], it[None]


def solution(mesh):
    placed = (
        P("sec", "row", None),
        P("sec", None, None),
        P("sec", "row", None),
        P("sec", None, None),
        P("sec", "row", None),
        P("sec", "row", None),
        P("sec", None),
        P("sec"),
        P("sec"),
        P("sec", None),
    )
    return jax.shard_map(
        local,
        mesh=mesh,
        in_specs=placed,
        out_specs=(P("sec", "row", None), P("sec", "row", None), P("sec", None, None)),
        check_vma=False,
    )
```

```python
import functools

import jax
import jax.numpy as jnp
from jax import lax
from jax.experimental import pallas as pl
from jax.experimental.pallas import tpu as pltpu
from jax.sharding import PartitionSpec as P

MESH = pl.DeviceIdType.MESH
F32 = jnp.float32
BF16 = jnp.bfloat16
LANES = 128
NT = (((1,), (1,)), ((), ()))


def chunk_list(tiles):
    sizes = [2] * (tiles // 2)
    return [(sum(sizes[:i]), size) for i, size in enumerate(sizes)]


def kernel(
    n_sec, n_row,
    ul, ur, dl, dr, lf, rf, sg, st, kp, jm,
    pt, pj, it,
    v_left, v_right, v_fac, v_sg, v_jm,
    gathered, outgoing, incoming, partial,
    right_sem, left_sem, fac_sem, jm_sem, sg_sem, g_send, g_recv, h_send, h_recv, i_send, i_recv,
):
    rows, width = ul.shape
    ks = lf.shape[0]
    chs = jm.shape[1]
    tiles = width // LANES
    chunks = chunk_list(tiles)
    sec = lax.axis_index("sec")
    row = lax.axis_index("row")
    near = (lax.rem(sec + 1, n_sec), lax.rem(sec + n_sec - 1, n_sec))
    offsets = sorted(range(1, n_row), key=lambda d: -min(d, n_row - d))

    def peer(offset):
        return lax.rem(row + offset, n_row)

    lefts, rights, factors = (ul, dl), (ur, dr), (lf, rf)
    rounds = [[(h, i - h) for h in range(2) if 0 <= i - h < len(chunks)] for i in range(len(chunks) + 1)]

    def columns(c):
        return pl.ds(chunks[c][0] * LANES, chunks[c][1] * LANES)

    def left_in(h):
        return pltpu.make_async_copy(lefts[h], v_left.at[h], left_sem.at[h])

    def held(h, tile, count):
        return pl.ds((tile + 2 * h) * LANES, count * LANES)

    def right_in(h, c):
        return pltpu.make_async_copy(
            rights[h].at[:, columns(c)], v_right.at[h, :, held(h, *chunks[c])], right_sem.at[c + h]
        )

    def round_in(parts):
        h, c = parts[0]
        landed = v_right.at[pl.ds(h, len(parts)), :, held(h, *chunks[c])]
        return pltpu.make_async_copy(landed, landed, right_sem.at[c + h])

    left_in(0).start()
    right_in(0, 0).start()
    barrier = pltpu.get_barrier_semaphore()
    for offset in offsets:
        pl.semaphore_signal(barrier, inc=1, device_id={"row": peer(offset)}, device_id_type=MESH)
    for other in near:
        pl.semaphore_signal(barrier, inc=1, device_id={"sec": other}, device_id_type=MESH)
    left_in(1).start()
    for h, c in rounds[1] + rounds[2]:
        right_in(h, c).start()
    for h in range(2):
        pltpu.make_async_copy(factors[h], v_fac.at[h], fac_sem).start()
    jm_in = pltpu.make_async_copy(jm, v_jm, jm_sem)
    sg_in = pltpu.make_async_copy(sg, v_sg, sg_sem)
    jm_in.start()
    sg_in.start()

    def iota(shape, axis):
        return lax.broadcasted_iota(jnp.int32, shape, axis)

    r_pick, c_pick = iota((2 * rows, rows), 0), iota((2 * rows, rows), 1)
    same = lax.rem(r_pick, rows) // chs == c_pick // chs
    z_pick = lax.rem(r_pick, chs)
    left_rows = r_pick < rows
    states = st[0]
    lane, sub = iota((rows, LANES), 1), iota((rows, LANES), 0)
    live = (lax.rem(lane, chs) < states) & (lax.rem(sub, chs) < states)
    low2 = lax.rem(iota((2 * chs, LANES), 1) // (2 * chs), 2) == 0
    low1 = lax.rem(iota((chs, LANES), 1) // chs, 2) == 0

    def swap_blocks(tile):
        a, b = tile[: 2 * chs], tile[2 * chs :]
        ab = (
            jnp.where(low2, a, pltpu.roll(b, 2 * chs, 1)),
            jnp.where(low2, pltpu.roll(a, LANES - 2 * chs, 1), b),
        )
        out = []
        for half in ab:
            a, b = half[:chs], half[chs:]
            out.append(jnp.where(low1, a, pltpu.roll(b, chs, 1)))
            out.append(jnp.where(low1, pltpu.roll(a, LANES - chs, 1), b))
        return jnp.concatenate(out, axis=0)

    def own_factors():
        seq = jnp.concatenate([v_jm[...]] * (rows // chs), axis=1)
        picker = jnp.where(same & (z_pick == seq), 1.0, 0.0)
        moved = lax.dot_general(
            v_fac[0], jnp.where(left_rows, picker, 0.0).astype(BF16), NT, preferred_element_type=F32
        ) + lax.dot_general(
            v_fac[1], jnp.where(left_rows, 0.0, picker).astype(BF16), NT, preferred_element_type=F32
        )
        gathered[0] = moved.astype(BF16)

    def product(h, c, alone):
        if alone:
            first, count = chunks[c]
            return jnp.concatenate(
                [
                    jnp.dot(v_left[h], v_right[h, :, held(h, t, 1)], preferred_element_type=F32)
                    for t in range(first, first + count)
                ],
                axis=1,
            )
        return jnp.dot(v_left[h], v_right[h, :, held(h, *chunks[c])], preferred_element_type=F32)

    def finish(h, c, full):
        for i in range(chunks[c][1]):
            tile = jnp.where(live, full[:, i * LANES : (i + 1) * LANES], 0.0)
            outgoing[h, chunks[c][0] + i] = swap_blocks(tile).astype(BF16)

    last = len(chunks) - 1

    def arrival(h, c):
        return 0 if h else 1 + c // max(last, 1)

    def wait_half(h, first, count):
        landed = incoming.at[pl.ds(first, count), pl.ds(h * rows, rows)]
        pltpu.make_async_remote_copy(
            src_ref=landed, dst_ref=landed, send_sem=h_send, recv_sem=h_recv.at[arrival(h, first // 2)],
            device_id={"sec": near[h]}, device_id_type=MESH,
        ).wait_recv()

    def half_copy(h, c):
        return pltpu.make_async_remote_copy(
            src_ref=outgoing.at[h, pl.ds(*chunks[c])],
            dst_ref=incoming.at[pl.ds(*chunks[c]), pl.ds(h * rows, rows)],
            send_sem=h_send,
            recv_sem=h_recv.at[arrival(h, c)],
            device_id={"sec": near[h]},
            device_id_type=MESH,
        )

    def row_copy(buffer, send_sem, recv_sem, offset):
        return pltpu.make_async_remote_copy(
            src_ref=buffer.at[0],
            dst_ref=buffer.at[n_row - offset],
            send_sem=send_sem,
            recv_sem=recv_sem,
            device_id={"row": peer(offset)},
            device_id_type=MESH,
        )

    def all_rows(buffer, send_sem, recv_sem):
        others = buffer.at[pl.ds(1, n_row - 1)]
        return pltpu.make_async_remote_copy(
            src_ref=others, dst_ref=others, send_sem=send_sem, recv_sem=recv_sem,
            device_id={"row": peer(1)}, device_id_type=MESH,
        )

    for i, parts in enumerate(rounds):
        if i < 2:
            left_in(i).wait()
        round_in(parts).wait()
        if i == 0:
            for later in rounds[3:]:
                for h, c in later:
                    right_in(h, c).start()
        if i == 1:
            pltpu.make_async_copy(v_fac, v_fac, fac_sem).wait()
            jm_in.wait()
        fulls = [product(h, c, len(parts) == 1) for h, c in parts]
        if i == 1:
            own_factors()
        for (h, c), full in zip(parts, fulls):
            finish(h, c, full)
        if i == 0:
            pl.semaphore_wait(barrier, n_row - 1 + 2)
        for h, c in parts:
            half_copy(h, c).start()
        if i == 1:
            for offset in offsets:
                row_copy(gathered, g_send, g_recv, offset).start()

    sg_in.wait()
    w_row = jnp.where(iota((1, ks), 1) < kp[0], 1.0 / jnp.sqrt(v_sg[...]), 0.0)
    diagonal = iota((ks, ks), 0) == iota((ks, ks), 1)
    weight = jnp.sum(jnp.where(diagonal, jnp.broadcast_to(w_row, (ks, ks)), 0.0), axis=1, keepdims=True)

    all_rows(gathered, g_send, g_recv).wait_recv()
    upper_lanes = iota((2 * ks, LANES), 1) < rows

    def pair(t):
        a, b = (
            jnp.concatenate(
                [gathered[lax.rem(2 * i + g - row + n_row, n_row)].astype(F32) for g in range(2)], axis=0
            )
            for i in (t, t + 1)
        )
        return (
            jnp.where(upper_lanes, a, pltpu.roll(b, rows, 1)).astype(BF16),
            jnp.where(upper_lanes, pltpu.roll(a, rows, 1), b).astype(BF16),
        )

    pairs = [pair(first) for first, _ in chunks]

    def contract(h, c, total):
        first, count = chunks[c]
        rhs = incoming[pl.ds(first, count), pl.ds(h * rows, rows)].reshape(count * rows, LANES)
        return total + jnp.dot(pairs[c][h], rhs, preferred_element_type=F32)

    def parted(total):
        return jnp.where(upper_lanes[:ks], total[:ks], total[ks:]) * weight

    def folded(value):
        return value + pltpu.roll(value, rows, 1)

    def split(value):
        high = value.astype(BF16)
        return high, (value - high.astype(F32)).astype(BF16)

    totals = [jnp.zeros((2 * ks, LANES), F32)] * 2
    wait_half(1, 0, tiles)
    for c in range(len(chunks)):
        totals[1] = contract(1, c, totals[1])
    scaled_b = folded(parted(totals[1]))
    pj[...] = scaled_b[:, :rows].astype(BF16)
    groups = LANES // ks
    high_b, low_b = (jnp.concatenate([v] * groups, axis=0) for v in split(scaled_b))
    rhs_b = jnp.concatenate([high_b, low_b, high_b, low_b], axis=1)
    wait_half(0, 0, tiles - 2)
    for c in range(len(chunks)):
        if c == last:
            wait_half(0, tiles - 2, 2)
        totals[0] = contract(0, c, totals[0])
    parted_a = parted(totals[0])

    high_a, low_a = split(parted_a)
    wide = lax.dot_general(
        jnp.concatenate([high_a, high_a, low_a, low_a], axis=1), rhs_b, NT, preferred_element_type=F32
    )
    own = lax.rem(iota((ks, LANES), 0) + iota((ks, LANES), 1) // ks, groups) == 0
    wide = jnp.where(own, wide, 0.0)
    for i in range(ks // groups):
        partial[0, pl.ds(i, 1)] = jnp.sum(wide[i * groups : (i + 1) * groups], axis=0, keepdims=True)
    for offset in offsets:
        row_copy(partial, i_send, i_recv, offset).start()

    pt[...] = folded(parted_a)[:, :rows].astype(BF16)
    all_rows(gathered, g_send, g_recv).wait_send()
    pltpu.make_async_remote_copy(
        src_ref=outgoing, dst_ref=outgoing, send_sem=h_send, recv_sem=h_send,
        device_id={"sec": near[0]}, device_id_type=MESH,
    ).wait_send()
    all_rows(partial, i_send, i_recv).wait_recv()
    terms = [partial[i] for i in range(n_row)]
    while len(terms) > 1:
        terms = [a + b for a, b in zip(terms[::2], terms[1::2])]
    spread = jnp.concatenate(
        [
            pltpu.roll(jnp.broadcast_to(terms[0][i : i + 1], (groups, LANES)), 0, 1, stride=ks, stride_axis=0)
            for i in range(ks // groups)
        ],
        axis=0,
    )
    it[...] = spread[:, :ks] / jnp.sqrt(F32(width))
    all_rows(partial, i_send, i_recv).wait_send()


def put_kernel(pt, pj, it, pt_out, pj_out, it_out, sem):
    copies = [
        pltpu.make_async_copy(a, b, sem.at[i])
        for i, (a, b) in enumerate(((pt, pt_out), (pj, pj_out), (it, it_out)))
    ]
    for copy in copies:
        copy.start()
    for copy in copies:
        copy.wait()


def local(
    corner_ul, corner_ur, corner_dl, corner_dr, left_factor, right_factor, singular, states, kept, joining_map
):
    n_sec, n_row = lax.axis_size("sec"), lax.axis_size("row")
    rows, width = corner_ul.shape[1:]
    ks = left_factor.shape[2]
    chs = joining_map.shape[1]
    tiles = width // LANES
    chunks = len(chunk_list(tiles))
    dma = pltpu.SemaphoreType.DMA
    hbm = pl.BlockSpec(memory_space=pltpu.HBM)
    smem = pl.BlockSpec(memory_space=pltpu.SMEM)
    vmem = pl.BlockSpec(memory_space=pltpu.VMEM)
    shapes = (((ks, rows), BF16), ((ks, rows), BF16), ((ks, ks), F32))
    results = pl.pallas_call(
        functools.partial(kernel, n_sec, n_row),
        out_shape=tuple(pltpu.VMEM(*s) for s in shapes),
        in_specs=[hbm] * 7 + [smem] * 2 + [hbm],
        out_specs=(vmem,) * 3,
        scratch_shapes=[
            pltpu.VMEM((2, rows, width), BF16),
            pltpu.VMEM((2, width, width + 2 * LANES), BF16),
            pltpu.VMEM((2, ks, rows), BF16),
            pltpu.VMEM((1, ks), F32),
            pltpu.VMEM((1, chs), jnp.int32),
            pltpu.VMEM((n_row, ks, 2 * rows), BF16),
            pltpu.VMEM((2, tiles, rows, LANES), BF16),
            pltpu.VMEM((tiles, 2 * rows, LANES), BF16),
            pltpu.VMEM((n_row, ks * ks // LANES, LANES), F32),
            dma((chunks + 1,)),
            dma((2,)),
            dma,
            dma,
            dma,
            dma,
            dma,
            dma,
            dma((3,)),
            dma,
            dma,
        ],
        compiler_params=pltpu.CompilerParams(collective_id=0, has_side_effects=True),
    )(
        corner_ul[0], corner_ur[0], corner_dl[0], corner_dr[0],
        left_factor[0].T, right_factor[0].T,
        singular, states, kept, joining_map,
    )
    pt, pj, it = pl.pallas_call(
        put_kernel,
        out_shape=tuple(jax.ShapeDtypeStruct(*s) for s in shapes),
        in_specs=[vmem] * 3,
        out_specs=(hbm,) * 3,
        scratch_shapes=[dma((3,))],
    )(*(pltpu.with_memory_space_constraint(v, pltpu.VMEM) for v in results))
    return pt.T[None], pj.T[None], it[None]


def solution(mesh):
    placed = (
        P("sec", "row", None),
        P("sec", None, None),
        P("sec", "row", None),
        P("sec", None, None),
        P("sec", "row", None),
        P("sec", "row", None),
        P("sec", None),
        P("sec"),
        P("sec"),
        P("sec", None),
    )
    return jax.shard_map(
        local,
        mesh=mesh,
        in_specs=placed,
        out_specs=(P("sec", "row", None), P("sec", "row", None), P("sec", None, None)),
        check_vma=False,
    )
```
